32 devices in a mesh: gy: 8 (over z, core), gz: 4 (over y, x).
Axes of the slice: x: 2, y: 2, z: 4, core: 2. Of those that a mesh axis runs over, the one named last changes fastest.
Arguments:
- measured: float32 [4, 1024, 1024], P('gz', 'gy'), may hold values from -20 to 20
- point_spread: float32 [1024, 1024], P('gy'), may hold values from -0.005859375 to 0.005859375
- stencil_weights: float32 [3, 3, 3], replicated, may hold values from -0.9 to 0.9
- upstream: float32 [4, 1024, 1024], P('gz', 'gy'), may hold values from -6 to 6
Outputs:
- grad_measured: float32 [4, 1024, 1024], P('gz', 'gy')
- grad_stencil: float32 [3, 3, 3], replicated
The draws below stay inside these ranges and needn't reach their ends.
All inputs are finite; a program needn't handle non-finite values.
Results may differ from the reference program's by a relative error of at most 0.00021.
Values sent between devices are 32-bit elements; how exact they have to be, the bound alone decides.
A program may use at most 64 MiB of HBM per device.

```python
import math
import jax
import jax.numpy as jnp

X = 1024
Y = 1024
ITERS = 2
Z = 4


def draw_measured(key, part):
    subkeys = jax.random.split(jax.random.fold_in(key, 11), 1)
    plane_index = jnp.arange(Z, dtype=jnp.float32)[:, None, None]
    attenuation = jnp.exp(-math.log(3.0) * plane_index / max(Z - 1, 1))
    return jnp.clip(jax.random.normal(subkeys[0], (Z, Y, X), jnp.float32), -6.0, 6.0) * attenuation


def block_levels(key, shape, cuts, smallest, largest):
    gain, own = 1.0, jax.random.fold_in(key, 6)
    for dim, blocks in cuts:
        heights = jnp.exp(jax.random.uniform(jax.random.fold_in(own, dim), (blocks,), jnp.float32, smallest / len(cuts), largest / len(cuts)))
        gain = gain * jnp.repeat(heights, shape[dim] // blocks).reshape([-1 if axis == dim else 1 for axis in range(len(shape))])
    return gain


def normal_values(own_key, extent, deviation, bound, pieces=(), kind=jnp.bfloat16):
    values = deviation * jax.random.normal(own_key, extent, jnp.float32)
    if pieces:
        values = values * block_levels(own_key, extent, pieces, -0.22, 0.18)
    return jnp.clip(values, -bound, bound).astype(kind)


def setup_inputs(seed: int = 0) -> dict:
    key_of = jax.random.split(jax.random.key(seed), 5)
    measured = draw_measured(jax.random.fold_in(key_of[4], 71), 0)
    point_spread = normal_values(key_of[1], (Y, X), (X * Y) ** -0.5, 0.005859375, ((0, 8),), jnp.float32)
    stencil_weights = normal_values(key_of[2], (3, 3, 3), 0.15, 0.9, (), jnp.float32)
    upstream = normal_values(key_of[3], (Z, Y, X), 1.0, 6.0, ((0, 4), (1, 8)), jnp.float32)
    return dict(measured=measured, point_spread=point_spread, stencil_weights=stencil_weights, upstream=upstream)


def apply_stencil(volume, kernel):
    planes, row_count, columns = volume.shape
    padded = jnp.pad(volume, 1)
    summed = jnp.zeros(volume.shape, jnp.float32)
    for shift_z in range(3):
        for shift_y in range(3):
            for shift_x in range(3):
                summed = summed + kernel[shift_z, shift_y, shift_x] * padded[shift_z:shift_z + planes, shift_y:shift_y + row_count, shift_x:shift_x + columns]
    return summed

def regularize(volume, kernel):
    mapped = apply_stencil(volume, kernel)
    return apply_stencil(mapped, kernel[::-1, ::-1, ::-1])

def filtered(volume, response):
    spectrum = jnp.fft.fft2(volume, axes=(1, 2))
    return jnp.real(jnp.fft.ifft2(spectrum * response, axes=(1, 2))).astype(jnp.float32)

def restore(measured, kernel, transfer):
    power_gain = jnp.real(transfer) ** 2 + jnp.imag(transfer) ** 2
    right_side = filtered(measured, jnp.conj(transfer))
    solution = jnp.zeros_like(right_side)
    residual = right_side
    direction = right_side
    norm_now = jnp.sum(residual * residual)
    for iteration in range(ITERS):
        applied = filtered(direction, power_gain) + regularize(direction, kernel)
        step_size = norm_now / jnp.sum(direction * applied)
        solution = solution + step_size * direction
        if iteration + 1 < ITERS:
            residual = residual - step_size * applied
            norm_next = jnp.sum(residual * residual)
            direction = residual + norm_next / norm_now * direction
            norm_now = norm_next
    return solution

def reference(measured, point_spread, stencil_weights, upstream):
    transfer = jnp.fft.fft2(point_spread)

    def forward(values, weights):
        return restore(values, weights, transfer)
    unused, pullback = jax.vjp(forward, measured, stencil_weights)
    grad_measured, grad_weights = pullback(upstream)
    return (grad_measured, grad_weights / math.sqrt(X * Y * Z))
```

```python
import math

import jax
import jax.numpy as jnp
from jax import lax
from jax.experimental import pallas as pl
from jax.experimental.pallas import tpu as pltpu
from jax.sharding import PartitionSpec as P

MESH = pl.DeviceIdType.MESH
SIDES = [(dy, dz) for dy in (-1, 0, 1) for dz in (-1, 0, 1) if (dy, dz) != (0, 0)]
VMEM = pl.BlockSpec(memory_space=pltpu.VMEM)
SMEM = pl.BlockSpec(memory_space=pltpu.SMEM)


def moved(value, shift):
    if shift == 0:
        return value
    width = value.shape[1]
    lane = lax.broadcasted_iota(jnp.int32, value.shape, 1)
    edge = 0 if shift > 0 else width - 1
    return jnp.where(lane == edge, 0.0, pltpu.roll(value, shift % width, 1))


def regular_kernel(count_y, count_z, weights, volume, back, grown, mapped, shifted, send, receive):
    rows, columns = volume.shape
    y, z = (lax.axis_index("gy"), lax.axis_index("gz"))

    def there(dy, dz):
        return (y + dy >= 0) & (y + dy < count_y) & (z + dz >= 0) & (z + dz < count_z)

    barrier = pltpu.get_barrier_semaphore()
    for dy, dz in SIDES:

        @pl.when(there(dy, dz))
        def _():
            pl.semaphore_signal(barrier, inc=1, device_id=(y + dy, z + dz), device_id_type=MESH)

    def span(place, count):
        return 1 + jnp.where(place > 0, 1, 0) + jnp.where(place < count - 1, 1, 0)

    pl.semaphore_wait(barrier, span(y, count_y) * span(z, count_z) - 1)

    def copy(field, phase, number):
        dy, dz = SIDES[number]
        source = field.at[1, pl.ds(rows if dy > 0 else 8, 8 if dy else rows)]
        start = 8 if dy == 0 else 0 if dy > 0 else rows + 8
        return pltpu.make_async_remote_copy(
            src_ref=source,
            dst_ref=field.at[1 - dz, pl.ds(start, 8 if dy else rows)],
            send_sem=send.at[phase, number],
            recv_sem=receive.at[phase, number],
            device_id=(y + dy, z + dz),
            device_id_type=MESH,
        )

    def exchange(field, phase):
        for number, (dy, dz) in enumerate(SIDES):

            @pl.when(there(dy, dz))
            def _():
                copy(field, phase, number).start()

        for number, (dy, dz) in enumerate(SIDES):
            start = 8 if dy == 0 else 0 if dy > 0 else rows + 8

            @pl.when(jnp.logical_not(there(-dy, -dz)))
            def _():
                field[1 - dz, pl.ds(start, 8 if dy else rows)] = jnp.zeros(
                    (8 if dy else rows, columns), jnp.float32
                )

        for number, (dy, dz) in enumerate(SIDES):

            @pl.when(there(-dy, -dz))
            def _():
                copy(field, phase, number).wait_recv()

            @pl.when(there(dy, dz))
            def _():
                copy(field, phase, number).wait_send()

    def apply(field, flip, put):
        def weight(a, b, c):
            return weights[26 - (9 * a + 3 * b + c) if flip else 9 * a + 3 * b + c]

        @pl.loop(0, (rows + 16) // 8)
        def _(step):
            here = pl.ds(pl.multiple_of(step * 8, 8), 8)
            sums = [None] * 3
            for a in range(3):
                value = field[a, here]
                for c in range(3):
                    turned = moved(value, 1 - c)
                    for b in range(3):
                        term = weight(a, b, c) * turned
                        sums[b] = term if sums[b] is None else sums[b] + term
            for b in range(3):
                shifted[b, here] = sums[b]

        @pl.loop(0, rows // 8)
        def _(step):
            first = pl.multiple_of(step * 8, 8)
            around = pl.ds(first, 24)
            total = shifted[1, pl.ds(first + 8, 8)]
            total = total + shifted[0, around][7:15] + shifted[2, around][9:17]
            put(first, total)

    @pl.loop(0, rows // 8)
    def _(step):
        first = pl.multiple_of(step * 8, 8)
        grown[1, pl.ds(first + 8, 8)] = volume[pl.ds(first, 8)]

    exchange(grown, 0)

    def put_mapped(first, total):
        mapped[1, pl.ds(first + 8, 8)] = total

    apply(grown, False, put_mapped)
    exchange(mapped, 1)

    def put_back(first, total):
        back[pl.ds(first, 8)] = total

    apply(mapped, True, put_back)


def regular(volume, kernel):
    rows, columns = volume.shape[1:]
    count_y, count_z = (lax.axis_size("gy"), lax.axis_size("gz"))
    field = jax.ShapeDtypeStruct((3, rows + 16, columns), jnp.float32)

    def body(*refs):
        regular_kernel(count_y, count_z, *refs)

    back, grown, mapped = pl.pallas_call(
        body,
        out_shape=(jax.ShapeDtypeStruct((rows, columns), jnp.float32), field, field),
        in_specs=[SMEM, VMEM],
        out_specs=(VMEM, VMEM, VMEM),
        scratch_shapes=[
            pltpu.VMEM((3, rows + 16, columns), jnp.float32),
            pltpu.SemaphoreType.DMA((2, 8)),
            pltpu.SemaphoreType.DMA((2, 8)),
        ],
        cost_estimate=pl.CostEstimate(flops=120 * rows * columns, bytes_accessed=20 * rows * columns, transcendentals=0),
        compiler_params=pltpu.CompilerParams(collective_id=0, has_side_effects=True),
        name="regular",
    )(kernel.reshape(27), volume[0])
    return (back[None], grown, mapped)


def total_kernel(count_y, count_z, value, out, column, row, across, send, receive):
    y, z = (lax.axis_index("gy"), lax.axis_index("gz"))
    along_y = [(lax.rem(y + k, count_y), z) for k in range(1, count_y)]
    along_z = [(y, lax.rem(z + k, count_z)) for k in range(1, count_z)]
    barrier = pltpu.get_barrier_semaphore()
    for place in along_y + along_z:
        pl.semaphore_signal(barrier, inc=1, device_id=place, device_id_type=MESH)
    pl.semaphore_wait(barrier, count_y + count_z - 2)

    def gather(source, slots, places, base):
        copies = []
        for k, place in enumerate(places):
            copies.append(
                pltpu.make_async_remote_copy(
                    src_ref=source,
                    dst_ref=slots.at[k],
                    send_sem=send.at[base + k],
                    recv_sem=receive.at[base + k],
                    device_id=place,
                    device_id_type=MESH,
                )
            )
            copies[-1].start()
        for item in copies:
            item.wait()

    def ordered(own, slots, index, count):
        total = jnp.zeros_like(own)
        for j in range(count):
            term = own
            for k in range(1, count):
                term = jnp.where(lax.rem(index - j + count, count) == k, slots[k - 1], term)
            total = total + term
        return total

    gather(value, column, along_y, 0)
    across[...] = ordered(value[...], column, y, count_y)
    gather(across, row, along_z, count_y - 1)
    out[...] = ordered(across[...], row, z, count_z)


def total(values, collective):
    count_y, count_z = (lax.axis_size("gy"), lax.axis_size("gz"))
    count = values.shape[0]

    def body(*refs):
        total_kernel(count_y, count_z, *refs)

    block = jnp.broadcast_to(jnp.pad(values, (0, 128 - count))[None], (8, 128))
    copies = count_y + count_z - 2
    summed = pl.pallas_call(
        body,
        out_shape=jax.ShapeDtypeStruct((8, 128), jnp.float32),
        in_specs=[VMEM],
        out_specs=VMEM,
        scratch_shapes=[
            pltpu.VMEM((count_y - 1, 8, 128), jnp.float32),
            pltpu.VMEM((count_z - 1, 8, 128), jnp.float32),
            pltpu.VMEM((8, 128), jnp.float32),
            pltpu.SemaphoreType.DMA((copies,)),
            pltpu.SemaphoreType.DMA((copies,)),
        ],
        compiler_params=pltpu.CompilerParams(collective_id=collective, has_side_effects=True),
        name="total",
    )(block)
    return summed[0, :count]


def correlate_kernel(scalars, grown_0, grown_1, grown_2, grown_up, mapped_0, mapped_1, mapped_2, mapped_up, out):
    rows = grown_0.shape[1] - 16
    columns = grown_0.shape[2]
    c_up, c_zero, c_one, c_two, d_zero, d_one, s_zero, s_grad, s_direction = (scalars[k] for k in range(9))
    out[...] = jnp.zeros_like(out)

    @pl.loop(0, rows // 8)
    def _(step):
        first = pl.multiple_of(step * 8, 8)
        here = pl.ds(first + 8, 8)
        zero, one = (mapped_0[1, here], mapped_1[1, here])
        grad = c_up * mapped_up[1, here] + c_zero * zero + c_one * one + c_two * mapped_2[1, here]
        values = (
            s_zero * zero + s_grad * grad,
            s_grad * zero,
            s_direction * (d_zero * zero + d_one * one),
        )
        turned = [[moved(value, c - 1) for value in values] for c in range(3)]
        for a in range(3):
            around = pl.ds(first, 24)
            full_0, full_1 = (grown_0[a, around], grown_1[a, around])
            full_grad = c_up * grown_up[a, around] + c_zero * full_0 + c_one * full_1 + c_two * grown_2[a, around]
            full_direction = d_zero * full_0 + d_one * full_1
            for b in range(3):
                fields = [item[7 + b : 15 + b] for item in (full_0, full_grad, full_direction)]
                for c in range(3):
                    product = turned[c][0] * fields[0] + turned[c][1] * fields[1] + turned[c][2] * fields[2]
                    folded = product[:, :128]
                    for part in range(1, columns // 128):
                        folded = folded + product[:, 128 * part : 128 * part + 128]
                    out[9 * a + 3 * b + c] += folded


def correlate(scalars, *fields):
    return pl.pallas_call(
        correlate_kernel,
        out_shape=jax.ShapeDtypeStruct((27, 8, 128), jnp.float32),
        in_specs=[SMEM] + [VMEM] * 8,
        out_specs=VMEM,
        cost_estimate=pl.CostEstimate(flops=40000000, bytes_accessed=8000000, transcendentals=0),
        name="correlate",
    )(scalars, *fields).sum((1, 2))


def contract(form, left, right):
    return jnp.einsum(form, left, right, precision=lax.Precision.HIGH)


def wave_tables(length, groups):
    half = length // 2
    bins = half // groups
    pair = groups // 2
    shape = (half, pair, 2, bins)
    place = lax.broadcasted_iota(jnp.int32, shape, 0)
    part = lax.broadcasted_iota(jnp.int32, shape, 2)
    slot = lax.broadcasted_iota(jnp.int32, shape, 1) * bins + lax.broadcasted_iota(jnp.int32, shape, 3)
    tables = []
    for odd in range(2):
        frequency = 2 * slot + odd
        steps = place * frequency + part * (length // 4)
        if not odd:
            steps = jnp.where((slot == 0) & (part == 1), place * half, steps)
        angle = (steps % length).astype(jnp.float32) * (2.0 * math.pi / length)
        tables.append(jnp.cos(angle).reshape(half, pair, 2 * bins))
    return tables


def combine(raw, on_row, on_lane):
    even, odd = raw
    a, b, c, d = (
        jnp.concatenate([piece[:, part, :, :, side] for piece in (even, odd)], 0)
        for part, side in ((0, 0), (0, 1), (1, 0), (1, 1))
    )
    special = on_row | on_lane
    plus_real = jnp.where(special, a, a - d)
    plus_imaginary = jnp.where(on_row, b, jnp.where(on_lane, c, b + c))
    minus_real = jnp.where(on_row, c, jnp.where(on_lane, b, a + d))
    minus_imaginary = jnp.where(special, d, b - c)
    return (jnp.stack([plus_real, minus_real]), jnp.stack([plus_imaginary, minus_imaginary]))


def separate(spectrum, on_row, on_lane):
    (plus_real, minus_real), (plus_imaginary, minus_imaginary) = spectrum
    special = on_row | on_lane
    a = jnp.where(special, plus_real, plus_real + minus_real)
    d = jnp.where(special, minus_imaginary, minus_real - plus_real)
    b = jnp.where(on_row, plus_imaginary, jnp.where(on_lane, minus_real, plus_imaginary + minus_imaginary))
    c = jnp.where(on_row, minus_real, jnp.where(on_lane, plus_imaginary, plus_imaginary - minus_imaginary))
    scale = jnp.where(on_row & on_lane, 1.0, 2.0)
    a, b, c, d = (value * scale for value in (a, b, c, d))
    whole = jnp.stack([jnp.stack([a, b], 3), jnp.stack([c, d], 3)], 1)
    pair = whole.shape[0] // 2
    return (whole[:pair], whole[pair:])


def times(left, right, corner, conjugate=False):
    (a, b), (c, d) = (left, right)
    cross = b * d
    sign = -1.0 if conjugate else 1.0
    real = jnp.where(corner, a * c, a * c - sign * cross)
    imaginary = jnp.where(corner, cross, sign * a * d + b * c)
    return (real, imaginary)


def linear(*terms):
    total_real = total_imaginary = 0.0
    for scale, (real, imaginary) in terms:
        scale_real, scale_imaginary = scale if isinstance(scale, tuple) else (scale, scale)
        total_real = total_real + scale_real * real
        total_imaginary = total_imaginary + scale_imaginary * imaginary
    return (total_real, total_imaginary)


def local(measured, point_spread, stencil_weights, upstream):
    planes, row_count, columns = measured.shape
    groups = lax.axis_size("gy")
    rows = row_count * groups
    cells = planes * rows * columns * lax.axis_size("gz")
    bins = columns // 2 // groups
    even_x, odd_x = wave_tables(columns, groups)
    even_y, odd_y = (even_x, odd_x) if rows == columns else wave_tables(rows, groups)
    y_bins = rows // 2 // groups
    spectral = (groups, y_bins, 1, bins)
    on_row = (lax.broadcasted_iota(jnp.int32, spectral, 0) == 0) & (
        lax.broadcasted_iota(jnp.int32, spectral, 1) == 0
    )
    on_lane = (lax.broadcasted_iota(jnp.int32, spectral, 3) == 0) & (lax.axis_index("gy") == 0)
    corner = on_row & on_lane

    def forward(volumes):
        count = volumes.shape[0]
        low, high = (volumes[:, :, : columns // 2], volumes[:, :, columns // 2 :])
        sent = jnp.concatenate(
            [contract("vrj,jdl->drvl", low + high, even_x), contract("vrj,jdl->drvl", low - high, odd_x)], 0
        )
        arrived = lax.all_to_all(
            sent.reshape(groups, row_count, count * 2 * bins), "gy", split_axis=0, concat_axis=0, tiled=True
        )
        arrived = arrived.reshape(rows, count * 2 * bins)
        low, high = (arrived[: rows // 2], arrived[rows // 2 :])
        raw = [
            contract("jds,jl->dsl", table, value).reshape(groups // 2, 2, y_bins, count, 2, bins)
            for table, value in ((even_y, low + high), (odd_y, low - high))
        ]
        return combine(raw, on_row, on_lane)

    def inverse(spectrum):
        count = spectrum[0].shape[3]
        pieces = separate(spectrum, on_row, on_lane)
        one, two = (
            contract("jds,dsl->jl", table, piece.reshape(groups // 2, 2 * y_bins, count * 2 * bins))
            for table, piece in ((even_y, pieces[0]), (odd_y, pieces[1]))
        )
        sent = jnp.concatenate([one + two, one - two], 0).reshape(groups, row_count, count * 2 * bins)
        arrived = lax.all_to_all(sent, "gy", split_axis=0, concat_axis=0, tiled=True)
        arrived = arrived.reshape(groups, row_count, count, 2 * bins)
        one = contract("drvl,jdl->vrj", arrived[: groups // 2], even_x)
        two = contract("drvl,jdl->vrj", arrived[groups // 2 :], odd_x)
        return jnp.concatenate([one + two, one - two], 2) / float(rows * columns)

    def pick(spectrum, start, count):
        return tuple(lax.slice_in_dim(part, start, start + count, axis=3) for part in spectrum)

    def join(*spectra):
        return tuple(jnp.concatenate(parts, 3) for parts in zip(*spectra))

    spectra = forward(jnp.concatenate([point_spread[None], measured], 0))
    transfer = pick(spectra, 0, 1)
    squares = (transfer[0] ** 2, transfer[1] ** 2)
    gain = (
        jnp.where(corner, squares[0], squares[0] + squares[1]),
        jnp.where(corner, squares[1], squares[0] + squares[1]),
    )
    spectrum_0 = times(pick(spectra, 1, planes), transfer, corner, True)
    blurred_0 = linear((gain, spectrum_0))
    pair = inverse(join(spectrum_0, blurred_0))
    vector_0 = pair[:planes]
    back_0, grown_0, mapped_0 = regular(vector_0, stencil_weights)
    back_up, grown_up, mapped_up = regular(upstream, stencil_weights)
    vector_1 = pair[planes:] + back_0
    spectrum_1 = linear((1.0, blurred_0), (1.0, forward(back_0)))
    blurred_1 = linear((gain, spectrum_1))
    early = forward(jnp.concatenate([upstream, back_up], 0))
    back_1, grown_1, mapped_1 = regular(vector_1, stencil_weights)
    vector_2 = inverse(blurred_1) + back_1
    norm_0, curve_0, image_0, up_0, up_1 = total(
        jnp.stack(
            [
                jnp.sum(vector_0 * vector_0),
                jnp.sum(vector_0 * vector_1),
                jnp.sum(vector_1 * vector_1),
                jnp.sum(upstream * vector_0),
                jnp.sum(upstream * vector_1),
            ]
        ),
        1,
    )
    step_0 = norm_0 / curve_0
    residual = vector_0 - step_0 * vector_1
    residual_image = vector_1 - step_0 * vector_2
    norm_1, cross, inner, up_residual, image_cross = total(
        jnp.stack(
            [
                jnp.sum(residual * residual),
                jnp.sum(residual * vector_1),
                jnp.sum(residual * residual_image),
                jnp.sum(upstream * residual),
                jnp.sum(residual_image * vector_1),
            ]
        ),
        2,
    )
    back_2, grown_2, mapped_2 = regular(vector_2, stencil_weights)
    late = forward(jnp.concatenate([back_1, back_2], 0))
    ratio = norm_1 / norm_0
    curve_1 = inner + 2.0 * ratio * cross + ratio * ratio * curve_0
    step_1 = norm_1 / curve_1
    grad_step_1 = up_residual + ratio * up_0
    grad_curve_1 = -grad_step_1 * step_1 / curve_1
    grad_ratio = step_1 * up_0 + 2.0 * grad_curve_1 * (cross + ratio * curve_0)
    known_image = step_1 * up_1 + 2.0 * grad_curve_1 * (image_cross + ratio * image_0)
    grad_norm = grad_step_1 / curve_1 + grad_ratio / norm_0
    grad_step_0 = up_0 - known_image - 2.0 * grad_norm * cross
    grad_curve_0 = -grad_step_0 * step_0 / curve_0
    grad_norm_0 = -grad_ratio * ratio / norm_0 + grad_step_0 / curve_0

    spectrum_2 = linear((1.0, linear((gain, spectrum_1))), (1.0, pick(late, 0, planes)))
    spectrum_up = pick(early, 0, planes)
    residual_terms = ((1.0, spectrum_0), (-step_0, spectrum_1))
    direction_image = linear((1.0 + ratio, spectrum_1), (-step_0, spectrum_2))
    grad_direction = linear((step_1, spectrum_up), (2.0 * grad_curve_1, direction_image))
    grad_residual = linear((1.0, grad_direction), (2.0 * grad_norm, linear(*residual_terms)))
    grad_back = linear(
        (step_1, pick(early, planes, planes)),
        (2.0 * grad_curve_1 * (1.0 + ratio) - 2.0 * grad_norm * step_0, pick(late, 0, planes)),
        (-2.0 * grad_curve_1 * step_0, pick(late, planes, planes)),
        (2.0 * grad_norm, linear((1.0, spectrum_1), (-1.0, blurred_0))),
    )
    grad_right = linear(
        (step_0, spectrum_up),
        (ratio, grad_direction),
        (2.0 * grad_curve_0, spectrum_1),
        (2.0 * grad_norm_0, spectrum_0),
        (1.0, grad_residual),
        (-step_0, linear((gain, grad_residual), (1.0, grad_back))),
    )
    grad_measured = inverse(times(grad_right, transfer, corner))

    terms = correlate(
        jnp.stack(
            [
                step_1,
                2.0 * grad_norm,
                2.0 * grad_curve_1 * (1.0 + ratio) - 2.0 * grad_norm * step_0,
                -2.0 * grad_curve_1 * step_0,
                1.0 + ratio,
                -step_0,
                2.0 * grad_curve_0,
                -step_0,
                2.0 * grad_curve_1,
            ]
        ),
        grown_0, grown_1, grown_2, grown_up, mapped_0, mapped_1, mapped_2, mapped_up,
    )
    grad_stencil = total(terms, 3).reshape(3, 3, 3) / math.sqrt(cells)
    return (grad_measured, grad_stencil)


def solution(mesh):
    return jax.shard_map(
        local,
        mesh=mesh,
        in_specs=(P("gz", "gy", None), P("gy", None), P(), P("gz", "gy", None)),
        out_specs=(P("gz", "gy", None), P()),
        check_vma=False,
    )
```
